32 devices in a mesh: lon: 2 (over x), lat: 16 (over z, y, core).
Axes of the slice: x: 2, y: 2, z: 4, core: 2. Of those that a mesh axis runs over, the one named last changes fastest.
Arguments:
- state: bfloat16 [1, 128, 256, 128], P(None, 'lat', 'lon'), may hold values from -6 to 6
- mix_weight: bfloat16 [128, 2, 128, 128], P('lat'), may hold values from -0.375 to 0.375
- skip_weight: bfloat16 [128, 128], replicated, may hold values from -0.5 to 0.5
Outputs:
- output: bfloat16 [1, 128, 256, 128], P(None, 'lat', 'lon')
The draws below stay inside these ranges and needn't reach their ends.
All inputs are finite; a program needn't handle non-finite values.
Results may differ from the reference program's by a relative error of at most 0.008.
Values may be sent and summed in bfloat16 or wider, within the bound.
A program may use at most 64 MiB of HBM per device.

```python
import math
import jax
import jax.numpy as jnp
from jax import lax

SAMPLES = 1
C = 128
NLAT = 128
NLON = 256
MODES = 128
DEGREES = 128


def block_levels(rng, shape, split, least, high):
    factor_of = 1.0
    for dim, parts in split:
        draws = jax.random.uniform(jax.random.fold_in(jax.random.fold_in(rng, 6), dim), (parts,), jnp.float32, least / len(split), high / len(split))
        factor_of = factor_of * jnp.repeat(jnp.exp(draws), shape[dim] // parts).reshape((-1,) + (1,) * (len(shape) - 1 - dim))
    return factor_of


def scatter_about(key, dims, scale, reach, shards=(), held_as=jnp.bfloat16):
    loudness = block_levels(key, dims, shards, -0.22, 0.18) if shards else 1.0
    entries = jax.random.normal(key, dims, jnp.float32) * scale * loudness
    return jnp.minimum(jnp.maximum(entries, -reach), reach).astype(held_as)


def setup_inputs(seed: int = 0) -> dict:
    key_list = jax.random.split(jax.random.key(seed), 4)
    state = scatter_about(key_list[0], (SAMPLES, NLAT, NLON, C), 1.0, 6.0, ((1, 16), (2, 2)))
    mix_weight = scatter_about(key_list[1], (DEGREES, 2, C, C), (2 * C) ** -0.5, 0.375, ((0, 16),))
    skip_weight = scatter_about(key_list[2], (C, C), C ** -0.5, 0.5)
    return dict(state=state, mix_weight=mix_weight, skip_weight=skip_weight)


rescale_limit = 1e+18
log_rescale = 18.0 * math.log(10.0)

def lat_geometry(lat_count):
    positions = jnp.arange(lat_count, dtype=jnp.float32)
    colatitude = jnp.pi * (positions + 0.5) / lat_count
    return (jnp.cos(colatitude), jnp.sin(colatitude))

def fourier_tables(lon_count, mode_count):
    lon_index = jnp.arange(lon_count, dtype=jnp.int32)[:, None]
    mode_index = jnp.arange(mode_count, dtype=jnp.int32)[None, :]
    angles = (lon_index * mode_index % lon_count).astype(jnp.float32) * (2.0 * math.pi / lon_count)
    norming = 1.0 / math.sqrt(lon_count)
    paired = jnp.stack([jnp.cos(angles), -jnp.sin(angles)], axis=2) * norming
    weight = jnp.where(mode_index == 0, 1.0, 2.0)[:, :, None]
    forward = paired.reshape(lon_count, 2 * mode_count).astype(jnp.bfloat16)
    backward = (paired * weight).reshape(lon_count, 2 * mode_count).astype(jnp.bfloat16)
    return (forward, backward)

def legendre_rows(mode_ids, lat_count, degrees):
    cosine, sine_values = lat_geometry(lat_count)
    orders = mode_ids.astype(jnp.float32)[:, None]
    counter = jnp.arange(1, degrees + 1, dtype=jnp.float32)
    halves = 0.5 * jnp.log((2.0 * counter + 1.0) / (2.0 * counter))
    summed = lax.optimization_barrier(jnp.sum(jnp.where(counter[None, :] <= orders, halves[None, :], jnp.float32(0.0)), axis=1, keepdims=True))
    log_start = 0.5 * jnp.log(jnp.float32(0.5)) + summed + orders * jnp.log(sine_values)[None, :]
    shape = (mode_ids.shape[0], lat_count)
    zeros = jnp.zeros(shape, jnp.float32)

    def advance(turn_index, carry):
        previous, earlier, exponent, collected = carry
        rows = []
        for offset in range(32):
            level = (turn_index * 32 + offset).astype(jnp.float32)
            ratio_a = jnp.sqrt(jnp.maximum(4.0 * level * level - 1.0, 0.0) / jnp.maximum(level * level - orders * orders, 1.0))
            below = level - 1.0
            ratio_b = jnp.sqrt(jnp.maximum(below * below - orders * orders, 0.0) / jnp.maximum(4.0 * below * below - 1.0, 1.0))
            raised = ratio_a * (cosine[None, :] * previous - ratio_b * earlier)
            at_start = level == orders
            current = jnp.where(at_start, 1.0, jnp.where(level > orders, raised, 0.0))
            exponent = jnp.where(at_start, log_start, exponent)
            oversize = jnp.abs(current) > rescale_limit
            factor = jnp.where(oversize, 1.0 / rescale_limit, 1.0)
            earlier = previous * factor
            previous = current * factor
            exponent = exponent + jnp.where(oversize, log_rescale, 0.0)
            rows.append(previous * jnp.exp(exponent))
        block_rows = jnp.stack(rows, axis=0)
        start_row = (turn_index * 32).astype(jnp.int32)
        collected = lax.dynamic_update_slice(collected, block_rows, (start_row, jnp.int32(0), jnp.int32(0)))
        return (previous, earlier, exponent, collected)
    initial = (zeros, zeros, zeros, jnp.zeros((degrees,) + shape, jnp.float32))
    return lax.fori_loop(0, degrees // 32, advance, initial)[3]

def mixing_blocks(mix_weight):
    real_part = mix_weight[:, 0]
    imag_part = mix_weight[:, 1]
    upper = jnp.concatenate([real_part, imag_part], axis=2)
    lower = jnp.concatenate([-imag_part, real_part], axis=2)
    return jnp.concatenate([upper, lower], axis=1)

def reference(state, mix_weight, skip_weight):
    forward, backward = fourier_tables(NLON, MODES)
    spectrum = jnp.einsum('sjkc,kq->sjqc', state.astype(jnp.float32), forward.astype(jnp.float32)).astype(jnp.bfloat16)
    block_weight = mixing_blocks(mix_weight).astype(jnp.float32)
    cosine, sine_values = lat_geometry(NLAT)
    group_size = 16

    def one_group(group_index):
        mode_ids = (group_index * group_size + jnp.arange(group_size, dtype=jnp.int32)).astype(jnp.int32)
        legendre = legendre_rows(mode_ids, NLAT, DEGREES)
        analysis = (legendre * (math.pi / math.sqrt(NLAT)) * sine_values[None, None, :]).astype(jnp.bfloat16)
        synthesis = (legendre * (1.0 / math.sqrt(DEGREES))).astype(jnp.bfloat16)
        start_col = (group_index * 2 * group_size).astype(jnp.int32)
        pieces = lax.dynamic_slice_in_dim(spectrum, start_col, 2 * group_size, axis=2)
        pieces = pieces.reshape(SAMPLES, NLAT, group_size, 2, C)
        coeffs = jnp.einsum('lij,sjirc->slirc', analysis.astype(jnp.float32), pieces.astype(jnp.float32)).astype(jnp.bfloat16)
        coeffs = coeffs.reshape(SAMPLES, DEGREES, group_size, 2 * C)
        mixed = jnp.einsum('slix,lxy->sliy', coeffs.astype(jnp.float32), block_weight).astype(jnp.bfloat16)
        gridded = jnp.einsum('lij,sliy->sjiy', synthesis.astype(jnp.float32), mixed.astype(jnp.float32)).astype(jnp.bfloat16)
        return gridded
    collected = lax.map(one_group, jnp.arange(MODES // group_size, dtype=jnp.int32))
    grid_modes = jnp.transpose(collected, (1, 2, 0, 3, 4)).reshape(SAMPLES, NLAT, 2 * MODES, C)
    spectral = jnp.einsum('sjqc,kq->sjkc', grid_modes.astype(jnp.float32), backward.astype(jnp.float32)).astype(jnp.bfloat16)
    local_term = jnp.einsum('sjkc,cd->sjkd', state.astype(jnp.float32), skip_weight.astype(jnp.float32))
    return jax.nn.gelu(spectral.astype(jnp.float32) + local_term).astype(jnp.bfloat16)
```

```python
import functools
import math

import jax
import jax.numpy as jnp
from jax import lax
from jax.experimental import pallas as pl
from jax.experimental.pallas import tpu as pltpu
from jax.sharding import PartitionSpec as P

MESH = pl.DeviceIdType.MESH
rescale_limit = 1e18
log_rescale = 18.0 * math.log(10.0)
F32 = jnp.float32
BF16 = jnp.bfloat16


def modulo(value, size):
    return value & (size - 1) if size & (size - 1) == 0 else lax.rem(value, size)


def fourier_values(mode_index, part, lon_index, lon_count):
    phase = modulo(lon_index * mode_index + part * (lon_count // 4), lon_count)
    return jnp.cos(phase.astype(F32) * (2.0 * math.pi / lon_count)) * (1.0 / math.sqrt(lon_count))


def build_forward(ft, lon_count, block):
    rows, columns = ft.shape

    def fill(step, carry):
        start = pl.multiple_of(step * block, block)
        q = lax.broadcasted_iota(jnp.int32, (block, columns), 0) + start
        k = lax.broadcasted_iota(jnp.int32, (block, columns), 1)
        ft[pl.ds(start, block), :] = fourier_values(q >> 1, q & 1, k, lon_count).astype(BF16)
        return carry

    lax.fori_loop(0, rows // block, fill, 0)


def build_backward(bt, lon_count, block):
    rows, columns = bt.shape

    def fill(step, carry):
        start = pl.multiple_of(step * block, block)
        k = lax.broadcasted_iota(jnp.int32, (block, columns), 0) + start
        q = lax.broadcasted_iota(jnp.int32, (block, columns), 1)
        weight = jnp.where(q < 2, 1.0, 2.0)
        bt[pl.ds(start, block), :] = (fourier_values(q >> 1, q & 1, k, lon_count) * weight).astype(BF16)
        return carry

    lax.fori_loop(0, rows // block, fill, 0)


def build_legendre(lg, an, syt, first_mode):
    own, degrees, lat_count = lg.shape
    shape = (own, lat_count)
    position = lax.broadcasted_iota(jnp.int32, (1, lat_count), 1).astype(F32)
    colatitude = math.pi * (position + 0.5) / lat_count
    cosine = jnp.cos(colatitude)
    sine = jnp.sin(colatitude)
    orders = (lax.broadcasted_iota(jnp.int32, shape, 0) + first_mode).astype(F32)
    counter = (lax.broadcasted_iota(jnp.int32, (own, degrees), 1) + 1).astype(F32)
    own_order = (lax.broadcasted_iota(jnp.int32, (own, degrees), 0) + first_mode).astype(F32)
    halves = 0.5 * jnp.log((2.0 * counter + 1.0) / (2.0 * counter))
    summed = jnp.sum(jnp.where(counter <= own_order, halves, 0.0), axis=1, keepdims=True)
    log_start = 0.5 * math.log(0.5) + summed + orders * jnp.log(sine)
    squares = orders * orders
    wide_cosine = jnp.broadcast_to(cosine, shape)
    unroll = 8

    def advance(step, carry):
        previous, earlier, exponent = carry
        for offset in range(unroll):
            index = step * unroll + offset
            level = jnp.full(shape, index, jnp.int32).astype(F32)
            ratio_a = jnp.sqrt(
                jnp.maximum(4.0 * level * level - 1.0, 0.0) / jnp.maximum(level * level - squares, 1.0)
            )
            below = level - 1.0
            ratio_b = jnp.sqrt(
                jnp.maximum(below * below - squares, 0.0)
                / jnp.maximum(4.0 * below * below - 1.0, 1.0)
            )
            raised = ratio_a * (wide_cosine * previous - ratio_b * earlier)
            at_start = level == orders
            current = jnp.where(at_start, 1.0, jnp.where(level > orders, raised, 0.0))
            exponent = jnp.where(at_start, log_start, exponent)
            oversize = jnp.abs(current) > rescale_limit
            factor = jnp.where(oversize, 1.0 / rescale_limit, 1.0)
            earlier = previous * factor
            previous = current * factor
            exponent = exponent + jnp.where(oversize, log_rescale, 0.0)
            value = previous * jnp.exp(exponent)
            for i in range(own):
                lg[i, pl.ds(index, 1), :] = value[i : i + 1]
        return previous, earlier, exponent

    zeros = jnp.zeros(shape, F32)
    lax.fori_loop(0, degrees // unroll, advance, (zeros, zeros, zeros))
    for i in range(own):
        value = lg[i]
        an[i] = (value * (math.pi / math.sqrt(lat_count)) * sine).astype(BF16)
        syt[i] = jnp.transpose(value * (1.0 / math.sqrt(degrees))).astype(BF16)


def gelu(v):
    return 0.5 * v * (1.0 + jnp.tanh(math.sqrt(2.0 / math.pi) * (v + 0.044715 * v * v * v)))


def kernel(
    L, G, state, mix, skip, out,
    st, mx, sk, ra, sb, rb, sc, rc, sd, rd, se, re, sf, rf,
    ft, bt, lg, an, syt, wb, scr, scm, local,
    sem_in, sem_own, sem_a, sem_ra, sem_s, sem_r, sem_f, sem_rf,
):
    N = L * G
    J, KD, C = st.shape
    R = J // L
    D = mx.shape[0]
    K = KD * L
    own = lg.shape[0]
    Q = 2 * own * N
    LAT = J * G
    DEG = D * G
    a = lax.axis_index("lon")
    g = lax.axis_index("lat")
    n = g * L + a

    def place(p):
        return (lax.rem(p, L), p // L)

    loads = [
        pltpu.make_async_copy(state.at[0], st, sem_in.at[0]),
        pltpu.make_async_copy(mix, mx, sem_in.at[1]),
        pltpu.make_async_copy(skip, sk, sem_in.at[2]),
    ]
    barrier = pltpu.get_barrier_semaphore()

    def greet(off, carry):
        pl.semaphore_signal(barrier, inc=1, device_id=place(lax.rem(n + off, N)), device_id_type=MESH)
        return carry

    lax.fori_loop(1, N, greet, 0)
    own_rows = pltpu.make_async_copy(state.at[0, pl.ds(a * R, R)], ra.at[a], sem_own)
    own_rows.start()
    for load in loads:
        load.start()
    build_forward(ft, K, 32)
    pl.semaphore_wait(barrier, N - 1)

    def row_copy(off, r):
        b = lax.rem(a + off, L)
        return pltpu.make_async_remote_copy(
            src_ref=state.at[0, b * R + r], dst_ref=ra.at[a, r],
            send_sem=sem_a.at[off, r], recv_sem=sem_ra.at[off, r],
            device_id=(b, g), device_id_type=MESH,
        )

    for r in range(R):
        for off in range(1, L):
            row_copy(off, r).start()
    own_rows.wait()
    for r in range(R):
        for off in range(1, L):
            row_copy(off, r).wait_recv()
        rows = ra[:, r].reshape(K, C)
        spectrum = jnp.dot(ft[...], rows, preferred_element_type=F32)
        sb[:, r] = spectrum.reshape(N, 2 * own, C).astype(BF16)

    def spread(stage, src, dst, count, me, target):
        def send(off, carry):
            p = lax.rem(me + off, count)
            pltpu.make_async_remote_copy(
                src_ref=src.at[p], dst_ref=dst.at[me],
                send_sem=sem_s.at[stage], recv_sem=sem_r.at[stage],
                device_id=target(p), device_id_type=MESH,
            ).start()
            return carry

        lax.fori_loop(1, count, send, 0)
        dst[me] = src[me]

    def gathered(stage, dst, count):
        part = dst.at[pl.ds(0, count - 1)]
        pltpu.make_async_copy(part, part, sem_r.at[stage]).wait()

    def drained(stage, src, count):
        part = src.at[pl.ds(0, count - 1)]
        pltpu.make_async_copy(part, part, sem_s.at[stage]).wait()

    spread(0, sb, rb, N, n, place)
    build_legendre(lg, an, syt, n * own)
    gathered(0, rb, N)
    scr[...] = rb[...].astype(F32).reshape(LAT * 2 * own, C)
    for i in range(own):
        pieces = jnp.concatenate(
            [scr[pl.ds(2 * i + part, LAT, stride=2 * own), :] for part in range(2)], axis=1
        ).astype(BF16)
        coeffs = jnp.dot(an[i], pieces, preferred_element_type=F32)
        for part in range(2):
            sc[:, i, part] = coeffs[:, part * C : (part + 1) * C].reshape(G, D, C).astype(BF16)

    def in_plane(h):
        return (a, h)

    spread(1, sc, rc, G, g, in_plane)
    for load in loads:
        load.wait()
    for l in range(D):
        wb[l, :C, :C] = mx[l, 0]
        wb[l, :C, C:] = mx[l, 1]
        wb[l, C:, :C] = -mx[l, 1]
        wb[l, C:, C:] = mx[l, 0]
    build_backward(bt, K, 32)
    gathered(1, rc, G)
    scm[0] = rc[...].astype(F32).reshape(DEG * own * 2, C)
    for l in range(D):
        paired = jnp.concatenate(
            [scm[0, pl.ds(part * D + l, G * own, stride=2 * D), :] for part in range(2)], axis=1
        ).astype(BF16)
        mixed = jnp.dot(paired, wb[l], preferred_element_type=F32)
        for part in range(2):
            scm[1, pl.ds(part * D + l, G * own, stride=2 * D), :] = mixed[:, part * C : (part + 1) * C]
    sd[...] = scm[1].reshape(G, own, 2, D, C).astype(BF16)

    spread(2, sd, rd, G, g, in_plane)
    for j in range(J):
        local[j] = jnp.dot(st[j], sk[...], preferred_element_type=F32)
    gathered(2, rd, G)
    for i in range(own):
        pieces = jnp.concatenate([rd[:, i, part].reshape(DEG, C) for part in range(2)], axis=1)
        gridded = jnp.dot(syt[i], pieces, preferred_element_type=F32)
        for part in range(2):
            scr[pl.ds(2 * i + part, LAT, stride=2 * own), :] = gridded[:, part * C : (part + 1) * C]
    se[...] = scr[...].reshape(N, R, 2 * own, C).astype(BF16)

    spread(3, se, re, N, n, place)
    gathered(3, re, N)

    def sector_copy(off, r):
        b = lax.rem(a + off, L)
        return pltpu.make_async_remote_copy(
            src_ref=sf.at[b, r], dst_ref=rf.at[a, r],
            send_sem=sem_f.at[off, r], recv_sem=sem_rf.at[off, r],
            device_id=(b, g), device_id_type=MESH,
        )

    def inverse(b, r):
        table = bt[pl.ds(pl.multiple_of(b * KD, KD), KD), :]
        modes = re[:, r].reshape(Q, C)
        return jnp.dot(table, modes, preferred_element_type=F32).astype(BF16)

    for r in range(R):
        for off in range(1, L):
            b = lax.rem(a + off, L)
            sf[b, r] = inverse(b, r)
            sector_copy(off, r).start()
    for r in range(R):
        row = a * R + r
        out[0, row] = gelu(inverse(a, r).astype(F32) + local[row]).astype(BF16)
    for r in range(R):
        for off in range(1, L):
            b = lax.rem(a + L - off, L)
            sector_copy(off, r).wait_recv()
            row = b * R + r
            out[0, row] = gelu(rf[b, r].astype(F32) + local[row]).astype(BF16)

    for r in range(R):
        for off in range(1, L):
            row_copy(off, r).wait_send()
            sector_copy(off, r).wait_send()
    drained(0, sb, N)
    drained(1, sc, G)
    drained(2, sd, G)
    drained(3, se, N)


def shards(state, mix_weight, skip_weight):
    samples, J, KD, C = state.shape
    D = mix_weight.shape[0]
    L = lax.axis_size("lon")
    G = lax.axis_size("lat")
    N, R, K, LAT, DEG = L * G, J // L, KD * L, J * G, D * G
    own = K // 2 // N
    Q = 2 * own * N
    wide = (N, R, 2 * own, C)
    deep = (G, own, 2, D, C)
    VMEM = pltpu.VMEM
    DMA = pltpu.SemaphoreType.DMA
    return pl.pallas_call(
        functools.partial(kernel, L, G),
        out_shape=jax.ShapeDtypeStruct(state.shape, BF16),
        in_specs=[pl.BlockSpec(memory_space=pl.ANY)] * 3,
        out_specs=pl.BlockSpec(memory_space=pltpu.VMEM),
        scratch_shapes=[
            VMEM((J, KD, C), BF16),
            VMEM(mix_weight.shape, BF16),
            VMEM((C, C), BF16),
            VMEM((L, R, KD, C), BF16),
            VMEM(wide, BF16), VMEM(wide, BF16),
            VMEM(deep, BF16), VMEM(deep, BF16),
            VMEM(deep, BF16), VMEM(deep, BF16),
            VMEM(wide, BF16), VMEM(wide, BF16),
            VMEM((L, R, KD, C), BF16), VMEM((L, R, KD, C), BF16),
            VMEM((Q, K), BF16), VMEM((K, Q), BF16),
            VMEM((own, DEG, LAT), F32),
            VMEM((own, DEG, LAT), BF16), VMEM((own, LAT, DEG), BF16),
            VMEM((D, 2 * C, 2 * C), BF16),
            VMEM((LAT * 2 * own, C), F32),
            VMEM((2, DEG * own * 2, C), F32),
            VMEM((J, KD, C), F32),
            DMA((3,)), DMA, DMA((L, R)), DMA((L, R)),
            DMA((4,)), DMA((4,)), DMA((L, R)), DMA((L, R)),
        ],
        compiler_params=pltpu.CompilerParams(
            collective_id=0, has_side_effects=True, vmem_limit_bytes=48 * 1024 * 1024
        ),
    )(state, mix_weight, skip_weight)


def solution(mesh):
    placed = (P(None, "lat", "lon", None), P("lat", None, None, None), P())
    return jax.shard_map(
        shards, mesh=mesh, in_specs=placed, out_specs=P(None, "lat", "lon", None), check_vma=False
    )
```

```python
import functools
import math

import jax
import jax.numpy as jnp
from jax import lax
from jax.experimental import pallas as pl
from jax.experimental.pallas import tpu as pltpu
from jax.sharding import PartitionSpec as P

MESH = pl.DeviceIdType.MESH
rescale_limit = 1e18
log_rescale = 18.0 * math.log(10.0)
F32 = jnp.float32
BF16 = jnp.bfloat16


def modulo(value, size):
    return value & (size - 1) if size & (size - 1) == 0 else lax.rem(value, size)


def build_forward(ft, lon_count, block):
    rows, columns = ft.shape
    quarter = lon_count // 4

    def fill(step, carry):
        start = pl.multiple_of(step * block, block)
        q = lax.broadcasted_iota(jnp.int32, (block, columns), 0) + start
        k = lax.broadcasted_iota(jnp.int32, (block, columns), 1)
        phase = modulo(k * (q >> 1) + (q & 1) * quarter, lon_count)
        folded = quarter - jnp.minimum(phase, lon_count - phase)
        angle = folded.astype(F32) * (2.0 * math.pi / lon_count)
        square = angle * angle
        total = jnp.full_like(square, 1.0 / math.factorial(13))
        for power in (11, 9, 7, 5, 3, 1):
            sign = 1.0 if power % 4 == 1 else -1.0
            total = total * square + sign / math.factorial(power)
        ft[pl.ds(start, block), :] = (total * angle * (1.0 / math.sqrt(lon_count))).astype(BF16)
        return carry

    lax.fori_loop(0, rows // block, fill, 0)


def build_backward(bt, ft, block):
    rows = ft.shape[0]
    for start in range(0, rows, block):
        bt[:, start : start + block] = jnp.transpose(ft[start : start + block, :].astype(F32)).astype(BF16)


def build_legendre(lg, an, syt, first_mode):
    own, degrees, lat_count = lg.shape
    shape = (own, lat_count)
    position = lax.broadcasted_iota(jnp.int32, (1, lat_count), 1).astype(F32)
    colatitude = math.pi * (position + 0.5) / lat_count
    cosine = jnp.cos(colatitude)
    sine = jnp.sin(colatitude)
    orders = (lax.broadcasted_iota(jnp.int32, shape, 0) + first_mode).astype(F32)
    counter = (lax.broadcasted_iota(jnp.int32, (own, degrees), 1) + 1).astype(F32)
    own_order = (lax.broadcasted_iota(jnp.int32, (own, degrees), 0) + first_mode).astype(F32)
    halves = 0.5 * jnp.log((2.0 * counter + 1.0) / (2.0 * counter))
    summed = jnp.sum(jnp.where(counter <= own_order, halves, 0.0), axis=1, keepdims=True)
    log_start = 0.5 * math.log(0.5) + summed + orders * jnp.log(sine)
    squares = orders * orders
    wide_cosine = jnp.broadcast_to(cosine, shape)
    unroll = 8

    def advance(step, carry):
        previous, earlier, exponent = carry
        for offset in range(unroll):
            index = step * unroll + offset
            level = jnp.full(shape, index, jnp.int32).astype(F32)
            ratio_a = jnp.sqrt(
                jnp.maximum(4.0 * level * level - 1.0, 0.0) / jnp.maximum(level * level - squares, 1.0)
            )
            below = level - 1.0
            ratio_b = jnp.sqrt(
                jnp.maximum(below * below - squares, 0.0)
                / jnp.maximum(4.0 * below * below - 1.0, 1.0)
            )
            raised = ratio_a * (wide_cosine * previous - ratio_b * earlier)
            at_start = level == orders
            current = jnp.where(at_start, 1.0, jnp.where(level > orders, raised, 0.0))
            exponent = jnp.where(at_start, log_start, exponent)
            oversize = jnp.abs(current) > rescale_limit
            factor = jnp.where(oversize, 1.0 / rescale_limit, 1.0)
            earlier = previous * factor
            previous = current * factor
            exponent = exponent + jnp.where(oversize, log_rescale, 0.0)
            value = previous * jnp.exp(exponent)
            for i in range(own):
                lg[i, pl.ds(index, 1), :] = value[i : i + 1]
        return previous, earlier, exponent

    zeros = jnp.zeros(shape, F32)
    lax.fori_loop(0, degrees // unroll, advance, (zeros, zeros, zeros))
    for i in range(own):
        value = lg[i]
        an[i] = (value * (math.pi / math.sqrt(lat_count)) * sine).astype(BF16)
        weight = jnp.where(orders[i : i + 1] == 0.0, 1.0, 2.0)
        syt[i] = jnp.transpose((value * (1.0 / math.sqrt(degrees))) * weight).astype(BF16)


def gelu(v):
    return 0.5 * v * (1.0 + jnp.tanh(math.sqrt(2.0 / math.pi) * (v + 0.044715 * v * v * v)))


def kernel(
    L, G, state, mix, skip, out,
    st, mx, sk, ra, sb, rb, sc, rc, sd, rd, se, re, sf, rf,
    ft, bt, lg, an, syt, wb, scr, scm, local, ov,
    sem_out, sem_in, sem_own, sem_a, sem_ra, sem_s, sem_r, sem_f, sem_rf,
):
    N = L * G
    J, KD, C = st.shape
    R = J // L
    D = mx.shape[0]
    K = KD * L
    own = lg.shape[0]
    Q = 2 * own * N
    LAT = J * G
    DEG = D * G
    a = lax.axis_index("lon")
    g = lax.axis_index("lat")
    n = g * L + a

    def place(p):
        return (lax.rem(p, L), p // L)

    loads = [
        pltpu.make_async_copy(state.at[0], st, sem_in.at[0]),
        pltpu.make_async_copy(mix, mx, sem_in.at[1]),
        pltpu.make_async_copy(skip, sk, sem_in.at[2]),
    ]
    barrier = pltpu.get_barrier_semaphore()

    def greet(off, carry):
        pl.semaphore_signal(barrier, inc=1, device_id=place(lax.rem(n + off, N)), device_id_type=MESH)
        return carry

    lax.fori_loop(1, N, greet, 0)
    own_rows = pltpu.make_async_copy(state.at[0, pl.ds(a * R, R)], ra.at[a], sem_own)
    own_rows.start()
    for load in loads:
        load.start()
    build_forward(ft, K, 32)
    pl.semaphore_wait(barrier, N - 1)

    def row_copy(off, r):
        b = lax.rem(a + off, L)
        return pltpu.make_async_remote_copy(
            src_ref=state.at[0, b * R + r], dst_ref=ra.at[a, r],
            send_sem=sem_a.at[off, r], recv_sem=sem_ra.at[off, r],
            device_id=(b, g), device_id_type=MESH,
        )

    for r in range(R):
        for off in range(1, L):
            row_copy(off, r).start()
    own_rows.wait()
    for r in range(R):
        for off in range(1, L):
            row_copy(off, r).wait_recv()
        rows = ra[:, r].reshape(K, C)
        spectrum = jnp.dot(ft[...], rows, preferred_element_type=F32)
        sb[:, r] = spectrum.reshape(N, 2 * own, C).astype(BF16)

    def spread(stage, src, dst, count, me, target):
        def send(off, carry):
            p = lax.rem(me + off, count)
            pltpu.make_async_remote_copy(
                src_ref=src.at[p], dst_ref=dst.at[me],
                send_sem=sem_s.at[stage], recv_sem=sem_r.at[stage],
                device_id=target(p), device_id_type=MESH,
            ).start()
            return carry

        lax.fori_loop(1, count, send, 0)
        dst[me] = src[me]

    def gathered(stage, dst, count):
        part = dst.at[pl.ds(0, count - 1)]
        pltpu.make_async_copy(part, part, sem_r.at[stage]).wait()

    def drained(stage, src, count):
        part = src.at[pl.ds(0, count - 1)]
        pltpu.make_async_copy(part, part, sem_s.at[stage]).wait()

    spread(0, sb, rb, N, n, place)
    build_legendre(lg, an, syt, n * own)
    gathered(0, rb, N)
    scr[...] = rb[...].astype(F32).reshape(LAT * 2 * own, C)
    for i in range(own):
        pieces = jnp.concatenate(
            [scr[pl.ds(2 * i + part, LAT, stride=2 * own), :] for part in range(2)], axis=1
        ).astype(BF16)
        coeffs = jnp.dot(an[i], pieces, preferred_element_type=F32)
        for part in range(2):
            sc[:, i, part] = coeffs[:, part * C : (part + 1) * C].reshape(G, D, C).astype(BF16)

    def in_plane(h):
        return (a, h)

    spread(1, sc, rc, G, g, in_plane)
    for load in loads:
        load.wait()
    for l in range(D):
        wb[l, :C, :C] = mx[l, 0]
        wb[l, :C, C:] = mx[l, 1]
        wb[l, C:, :C] = -mx[l, 1]
        wb[l, C:, C:] = mx[l, 0]
    build_backward(bt, ft, 128)
    gathered(1, rc, G)
    scm[0] = rc[...].astype(F32).reshape(DEG * own * 2, C)
    for l in range(D):
        paired = jnp.concatenate(
            [scm[0, pl.ds(part * D + l, G * own, stride=2 * D), :] for part in range(2)], axis=1
        ).astype(BF16)
        mixed = jnp.dot(paired, wb[l], preferred_element_type=F32)
        for part in range(2):
            scm[1, pl.ds(part * D + l, G * own, stride=2 * D), :] = mixed[:, part * C : (part + 1) * C]
    sd[...] = scm[1].reshape(G, own, 2, D, C).astype(BF16)

    spread(2, sd, rd, G, g, in_plane)
    for j in range(J):
        local[j] = jnp.dot(st[j], sk[...], preferred_element_type=F32)
    gathered(2, rd, G)
    for i in range(own):
        pieces = jnp.concatenate([rd[:, i, part].reshape(DEG, C) for part in range(2)], axis=1)
        gridded = jnp.dot(syt[i], pieces, preferred_element_type=F32)
        for part in range(2):
            scr[pl.ds(2 * i + part, LAT, stride=2 * own), :] = gridded[:, part * C : (part + 1) * C]
    se[...] = scr[...].reshape(N, R, 2 * own, C).astype(BF16)

    spread(3, se, re, N, n, place)
    gathered(3, re, N)

    def sector_copy(off, r):
        b = lax.rem(a + off, L)
        return pltpu.make_async_remote_copy(
            src_ref=sf.at[b, r], dst_ref=rf.at[a, r],
            send_sem=sem_f.at[off, r], recv_sem=sem_rf.at[off, r],
            device_id=(b, g), device_id_type=MESH,
        )

    def inverse(b, r):
        table = bt[pl.ds(pl.multiple_of(b * KD, KD), KD), :]
        modes = re[:, r].reshape(Q, C)
        return jnp.dot(table, modes, preferred_element_type=F32).astype(BF16)

    def result_copy(off, b):
        rows = pl.ds(b * R, R)
        return pltpu.make_async_copy(ov.at[rows], out.at[0, rows], sem_out.at[off])

    for r in range(R):
        for off in range(1, L):
            b = lax.rem(a + off, L)
            sf[b, r] = inverse(b, r)
            sector_copy(off, r).start()
    for r in range(R):
        row = a * R + r
        ov[row] = gelu(inverse(a, r).astype(F32) + local[row]).astype(BF16)
    result_copy(0, a).start()
    for off in range(1, L):
        b = lax.rem(a + L - off, L)
        for r in range(R):
            sector_copy(off, r).wait_recv()
            row = b * R + r
            ov[row] = gelu(rf[b, r].astype(F32) + local[row]).astype(BF16)
        result_copy(off, b).start()

    for r in range(R):
        for off in range(1, L):
            row_copy(off, r).wait_send()
            sector_copy(off, r).wait_send()
    for off in range(L):
        result_copy(off, lax.rem(a + L - off, L)).wait()
    drained(0, sb, N)
    drained(1, sc, G)
    drained(2, sd, G)
    drained(3, se, N)


def shards(state, mix_weight, skip_weight):
    samples, J, KD, C = state.shape
    D = mix_weight.shape[0]
    L = lax.axis_size("lon")
    G = lax.axis_size("lat")
    N, R, K, LAT, DEG = L * G, J // L, KD * L, J * G, D * G
    own = K // 2 // N
    Q = 2 * own * N
    wide = (N, R, 2 * own, C)
    deep = (G, own, 2, D, C)
    VMEM = pltpu.VMEM
    DMA = pltpu.SemaphoreType.DMA
    return pl.pallas_call(
        functools.partial(kernel, L, G),
        out_shape=jax.ShapeDtypeStruct(state.shape, BF16),
        in_specs=[pl.BlockSpec(memory_space=pltpu.HBM)] * 3,
        out_specs=pl.BlockSpec(memory_space=pltpu.HBM),
        scratch_shapes=[
            VMEM((J, KD, C), BF16),
            VMEM(mix_weight.shape, BF16),
            VMEM((C, C), BF16),
            VMEM((L, R, KD, C), BF16),
            VMEM(wide, BF16), VMEM(wide, BF16),
            VMEM(deep, BF16), VMEM(deep, BF16),
            VMEM(deep, BF16), VMEM(deep, BF16),
            VMEM(wide, BF16), VMEM(wide, BF16),
            VMEM((L, R, KD, C), BF16), VMEM((L, R, KD, C), BF16),
            VMEM((Q, K), BF16), VMEM((K, Q), BF16),
            VMEM((own, DEG, LAT), F32),
            VMEM((own, DEG, LAT), BF16), VMEM((own, LAT, DEG), BF16),
            VMEM((D, 2 * C, 2 * C), BF16),
            VMEM((LAT * 2 * own, C), F32),
            VMEM((2, DEG * own * 2, C), F32),
            VMEM((J, KD, C), F32), VMEM((J, KD, C), BF16),
            DMA((L,)), DMA((3,)), DMA, DMA((L, R)), DMA((L, R)),
            DMA((4,)), DMA((4,)), DMA((L, R)), DMA((L, R)),
        ],
        compiler_params=pltpu.CompilerParams(
            collective_id=0, has_side_effects=True, vmem_limit_bytes=60 * 1024 * 1024
        ),
    )(state, mix_weight, skip_weight)


def solution(mesh):
    placed = (P(None, "lat", "lon", None), P("lat", None, None, None), P())
    return jax.shard_map(
        shards, mesh=mesh, in_specs=placed, out_specs=P(None, "lat", "lon", None), check_vma=False
    )
```

```python
import functools
import math

import jax
import jax.numpy as jnp
from jax import lax
from jax.experimental import pallas as pl
from jax.experimental.pallas import tpu as pltpu
from jax.sharding import PartitionSpec as P

MESH = pl.DeviceIdType.MESH
rescale_limit = 1e18
log_rescale = 18.0 * math.log(10.0)
F32 = jnp.float32
BF16 = jnp.bfloat16


def modulo(value, size):
    return value & (size - 1) if size & (size - 1) == 0 else lax.rem(value, size)


def build_forward(ft, lon_count, own, block):
    rows, columns = ft.shape
    quarter = lon_count // 4
    devices = rows // 2 // own

    def fill(step, carry):
        start = pl.multiple_of(step * block, block)
        q = lax.broadcasted_iota(jnp.int32, (block, columns), 0) + start
        k = lax.broadcasted_iota(jnp.int32, (block, columns), 1)
        mode = modulo(q >> 1, own) * devices + lax.div(q >> 1, own)
        phase = modulo(k * mode + (q & 1) * quarter, lon_count)
        folded = quarter - jnp.minimum(phase, lon_count - phase)
        angle = folded.astype(F32) * (2.0 * math.pi / lon_count)
        square = angle * angle
        total = jnp.full_like(square, 1.0 / math.factorial(13))
        for power in (11, 9, 7, 5, 3, 1):
            sign = 1.0 if power % 4 == 1 else -1.0
            total = total * square + sign / math.factorial(power)
        ft[pl.ds(start, block), :] = (total * angle * (1.0 / math.sqrt(lon_count))).astype(BF16)
        return carry

    lax.fori_loop(0, rows // block, fill, 0)


def build_backward(bt, ft, block):
    rows = ft.shape[0]
    for start in range(0, rows, block):
        bt[:, start : start + block] = jnp.transpose(ft[start : start + block, :].astype(F32)).astype(BF16)


def build_legendre(lg, an, syt, first_mode, stride):
    own, degrees, lat_count = lg.shape
    shape = (own, lat_count)
    position = lax.broadcasted_iota(jnp.int32, (1, lat_count), 1).astype(F32)
    colatitude = math.pi * (position + 0.5) / lat_count
    cosine = jnp.cos(colatitude)
    sine = jnp.sin(colatitude)
    orders = (lax.broadcasted_iota(jnp.int32, shape, 0) * stride + first_mode).astype(F32)
    counter = (lax.broadcasted_iota(jnp.int32, (own, degrees), 1) + 1).astype(F32)
    own_order = (lax.broadcasted_iota(jnp.int32, (own, degrees), 0) * stride + first_mode).astype(F32)
    halves = 0.5 * jnp.log((2.0 * counter + 1.0) / (2.0 * counter))
    summed = jnp.sum(jnp.where(counter <= own_order, halves, 0.0), axis=1, keepdims=True)
    log_start = 0.5 * math.log(0.5) + summed + orders * jnp.log(sine)
    squares = orders * orders
    wide_cosine = jnp.broadcast_to(cosine, shape)
    unroll = 8

    def advance(step, carry):
        previous, earlier, exponent = carry
        for offset in range(unroll):
            index = step * unroll + offset
            level = jnp.full(shape, index, jnp.int32).astype(F32)
            ratio_a = jnp.sqrt(
                jnp.maximum(4.0 * level * level - 1.0, 0.0) / jnp.maximum(level * level - squares, 1.0)
            )
            below = level - 1.0
            ratio_b = jnp.sqrt(
                jnp.maximum(below * below - squares, 0.0)
                / jnp.maximum(4.0 * below * below - 1.0, 1.0)
            )
            raised = ratio_a * (wide_cosine * previous - ratio_b * earlier)
            at_start = level == orders
            current = jnp.where(at_start, 1.0, jnp.where(level > orders, raised, 0.0))
            exponent = jnp.where(at_start, log_start, exponent)
            oversize = jnp.abs(current) > rescale_limit
            factor = jnp.where(oversize, 1.0 / rescale_limit, 1.0)
            earlier = previous * factor
            previous = current * factor
            exponent = exponent + jnp.where(oversize, log_rescale, 0.0)
            value = previous * jnp.exp(exponent)
            for i in range(own):
                lg[i, pl.ds(index, 1), :] = value[i : i + 1]
        return previous, earlier, exponent

    zeros = jnp.zeros(shape, F32)
    lax.fori_loop(0, degrees // unroll, advance, (zeros, zeros, zeros))
    for i in range(own):
        value = lg[i]
        an[i] = (value * (math.pi / math.sqrt(lat_count)) * sine).astype(BF16)
        weight = jnp.where(orders[i : i + 1] == 0.0, 1.0, 2.0)
        syt[i] = jnp.transpose((value * (1.0 / math.sqrt(degrees))) * weight).astype(BF16)


def chunk_modes(own):
    return own // 2 if own % 2 == 0 else own


def gelu(v):
    return 0.5 * v * (1.0 + jnp.tanh(math.sqrt(2.0 / math.pi) * (v + 0.044715 * v * v * v)))


def kernel(
    L, G, state, mix, skip, out,
    st, mx, sk, ra, sb, rb, sc, rc, sd, rd, se, re, sf, rf,
    ft, bt, lg, an, syt, wb, scr, scm, local, ov,
    sem_out, sem_in, sem_own, sem_a, sem_ra, sem_s, sem_r, sem_f, sem_rf,
    sem_cs, sem_cr, sem_ds, sem_dr,
):
    N = L * G
    J, KD, C = st.shape
    R = J // L
    D = mx.shape[0]
    K = KD * L
    own = lg.shape[0]
    Q = 2 * own * N
    LAT = J * G
    DEG = D * G
    a = lax.axis_index("lon")
    g = lax.axis_index("lat")
    n = g * L + a

    def place(p):
        return (lax.rem(p, L), p // L)

    loads = [
        pltpu.make_async_copy(state.at[0], st, sem_in.at[0]),
        pltpu.make_async_copy(mix, mx, sem_in.at[1]),
        pltpu.make_async_copy(skip, sk, sem_in.at[2]),
    ]
    rc[...] = jnp.zeros_like(rc)
    rd[...] = jnp.zeros_like(rd)
    barrier = pltpu.get_barrier_semaphore()

    def greet(off, carry):
        pl.semaphore_signal(barrier, inc=1, device_id=place(lax.rem(n + off, N)), device_id_type=MESH)
        return carry

    lax.fori_loop(1, N, greet, 0)
    own_rows = pltpu.make_async_copy(state.at[0, pl.ds(a * R, R)], ra.at[a], sem_own)
    own_rows.start()
    for load in loads:
        load.start()
    pl.semaphore_wait(barrier, N - 1)

    def row_copy(off, r):
        b = lax.rem(a + off, L)
        return pltpu.make_async_remote_copy(
            src_ref=state.at[0, b * R + r], dst_ref=ra.at[a, r],
            send_sem=sem_a.at[off, r], recv_sem=sem_ra.at[off, r],
            device_id=(b, g), device_id_type=MESH,
        )

    for r in range(R):
        for off in range(1, L):
            row_copy(off, r).start()
    build_forward(ft, K, own, 32)
    own_rows.wait()
    for r in range(R):
        for off in range(1, L):
            row_copy(off, r).wait_recv()
        rows = ra[:, r].reshape(K, C)
        spectrum = jnp.dot(ft[...], rows, preferred_element_type=F32)
        sb[:, r] = spectrum.reshape(N, 2 * own, C).astype(BF16)

    def spread(stage, src, dst, count, me, target):
        def send(off, carry):
            p = lax.rem(me + off, count)
            pltpu.make_async_remote_copy(
                src_ref=src.at[p], dst_ref=dst.at[me],
                send_sem=sem_s.at[stage], recv_sem=sem_r.at[stage],
                device_id=target(p), device_id_type=MESH,
            ).start()
            return carry

        lax.fori_loop(1, count, send, 0)
        dst[me] = src[me]

    def gathered(stage, dst, count):
        part = dst.at[pl.ds(0, count - 1)]
        pltpu.make_async_copy(part, part, sem_r.at[stage]).wait()

    def drained(stage, src, count):
        part = src.at[pl.ds(0, count - 1)]
        pltpu.make_async_copy(part, part, sem_s.at[stage]).wait()

    def wanted(i, h, d):
        return N * i + h * L + a <= D * d + D - 1

    def forth(i, h):
        return pltpu.make_async_remote_copy(
            src_ref=sc.at[i, h], dst_ref=rc.at[i, g],
            send_sem=sem_cs.at[i, h], recv_sem=sem_cr.at[i, g],
            device_id=(a, h), device_id_type=MESH,
        )

    def came_forth(i, h):
        return pltpu.make_async_copy(rc.at[i, h], rc.at[i, h], sem_cr.at[i, h])

    def went_forth(i, h):
        return pltpu.make_async_copy(sc.at[i, h], sc.at[i, h], sem_cs.at[i, h])

    def back(i, h):
        return pltpu.make_async_remote_copy(
            src_ref=sd.at[i, h], dst_ref=rd.at[i, g],
            send_sem=sem_ds.at[i, h], recv_sem=sem_dr.at[i, g],
            device_id=(a, h), device_id_type=MESH,
        )

    def came_back(i, h):
        return pltpu.make_async_copy(rd.at[i, h], rd.at[i, h], sem_dr.at[i, h])

    def went_back(i, h):
        return pltpu.make_async_copy(sd.at[i, h], sd.at[i, h], sem_ds.at[i, h])

    def start(copy, i, condition):
        def act(h):
            @pl.when(condition(h))
            def _():
                copy(i, h).start()
        return act

    def finish(copy, i, condition):
        def act(h):
            @pl.when(condition(h))
            def _():
                copy(i, h).wait()
        return act

    def each_other(act):
        def step(off, carry):
            act(lax.rem(g + off, G))
            return carry

        lax.fori_loop(1, G, step, 0)

    spread(0, sb, rb, N, n, place)
    build_legendre(lg, an, syt, n, N)
    gathered(0, rb, N)
    scr[...] = rb[...].astype(F32).reshape(LAT * 2 * own, C)
    for i in range(own):
        pieces = jnp.concatenate(
            [scr[pl.ds(2 * i + part, LAT, stride=2 * own), :] for part in range(2)], axis=1
        ).astype(BF16)
        coeffs = jnp.dot(an[i], pieces, preferred_element_type=F32)
        for part in range(2):
            sc[i, :, part] = coeffs[:, part * C : (part + 1) * C].reshape(G, D, C).astype(BF16)
        each_other(start(forth, i, lambda h: wanted(i, g, h)))
        rc[i, g] = sc[i, g]

    for load in loads:
        load.wait()
    for l in range(D):
        wb[l, :C, :C] = mx[l, 0]
        wb[l, :C, C:] = mx[l, 1]
        wb[l, C:, :C] = -mx[l, 1]
        wb[l, C:, C:] = mx[l, 0]
    size = chunk_modes(own)
    for first in range(0, own, size):
        for i in range(first, first + size):
            each_other(finish(came_forth, i, lambda h: wanted(i, h, g)))
        scm[0] = rc[first : first + size].astype(F32).reshape(size * G * 2 * D, C)
        for l in range(D):
            paired = jnp.concatenate(
                [scm[0, pl.ds(part * D + l, size * G, stride=2 * D), :] for part in range(2)], axis=1
            ).astype(BF16)
            mixed = jnp.dot(paired, wb[l], preferred_element_type=F32)
            for part in range(2):
                scm[1, pl.ds(part * D + l, size * G, stride=2 * D), :] = mixed[:, part * C : (part + 1) * C]
        sd[first : first + size] = scm[1].reshape(size, G, 2, D, C).astype(BF16)
        for i in range(first, first + size):
            each_other(start(back, i, lambda h: wanted(i, h, g)))
            rd[i, g] = sd[i, g]

    for j in range(J):
        local[j] = jnp.dot(st[j], sk[...], preferred_element_type=F32)
    build_backward(bt, ft, 128)
    for i in range(own):
        each_other(finish(came_back, i, lambda h: wanted(i, g, h)))
        pieces = jnp.concatenate([rd[i, :, part].reshape(DEG, C) for part in range(2)], axis=1)
        gridded = jnp.dot(syt[i], pieces, preferred_element_type=F32)
        for part in range(2):
            scr[pl.ds(2 * i + part, LAT, stride=2 * own), :] = gridded[:, part * C : (part + 1) * C]
    se[...] = scr[...].reshape(N, R, 2 * own, C).astype(BF16)

    spread(1, se, re, N, n, place)
    gathered(1, re, N)

    def sector_copy(off, r):
        b = lax.rem(a + off, L)
        return pltpu.make_async_remote_copy(
            src_ref=sf.at[b, r], dst_ref=rf.at[a, r],
            send_sem=sem_f.at[off, r], recv_sem=sem_rf.at[off, r],
            device_id=(b, g), device_id_type=MESH,
        )

    def inverse(b, r):
        table = bt[pl.ds(pl.multiple_of(b * KD, KD), KD), :]
        modes = re[:, r].reshape(Q, C)
        return jnp.dot(table, modes, preferred_element_type=F32).astype(BF16)

    def result_copy(off, b):
        rows = pl.ds(b * R, R)
        return pltpu.make_async_copy(ov.at[rows], out.at[0, rows], sem_out.at[off])

    for r in range(R):
        for off in range(1, L):
            b = lax.rem(a + off, L)
            sf[b, r] = inverse(b, r)
            sector_copy(off, r).start()
    for r in range(R):
        row = a * R + r
        ov[row] = gelu(inverse(a, r).astype(F32) + local[row]).astype(BF16)
    result_copy(0, a).start()
    for off in range(1, L):
        b = lax.rem(a + L - off, L)
        for r in range(R):
            sector_copy(off, r).wait_recv()
            row = b * R + r
            ov[row] = gelu(rf[b, r].astype(F32) + local[row]).astype(BF16)
        result_copy(off, b).start()

    for r in range(R):
        for off in range(1, L):
            row_copy(off, r).wait_send()
            sector_copy(off, r).wait_send()
    for off in range(L):
        result_copy(off, lax.rem(a + L - off, L)).wait()
    drained(0, sb, N)
    for i in range(own):
        each_other(finish(went_forth, i, lambda h: wanted(i, g, h)))
        each_other(finish(went_back, i, lambda h: wanted(i, h, g)))
    drained(1, se, N)


def shards(state, mix_weight, skip_weight):
    samples, J, KD, C = state.shape
    D = mix_weight.shape[0]
    L = lax.axis_size("lon")
    G = lax.axis_size("lat")
    N, R, K, LAT, DEG = L * G, J // L, KD * L, J * G, D * G
    own = K // 2 // N
    Q = 2 * own * N
    wide = (N, R, 2 * own, C)
    deep = (own, G, 2, D, C)
    VMEM = pltpu.VMEM
    DMA = pltpu.SemaphoreType.DMA
    return pl.pallas_call(
        functools.partial(kernel, L, G),
        out_shape=jax.ShapeDtypeStruct(state.shape, BF16),
        in_specs=[pl.BlockSpec(memory_space=pltpu.HBM)] * 3,
        out_specs=pl.BlockSpec(memory_space=pltpu.VMEM),
        scratch_shapes=[
            VMEM((J, KD, C), BF16),
            VMEM(mix_weight.shape, BF16),
            VMEM((C, C), BF16),
            VMEM((L, R, KD, C), BF16),
            VMEM(wide, BF16), VMEM(wide, BF16),
            VMEM(deep, BF16), VMEM(deep, BF16),
            VMEM(deep, BF16), VMEM(deep, BF16),
            VMEM(wide, BF16), VMEM(wide, BF16),
            VMEM((L, R, KD, C), BF16), VMEM((L, R, KD, C), BF16),
            VMEM((Q, K), BF16), VMEM((K, Q), BF16),
            VMEM((own, DEG, LAT), F32),
            VMEM((own, DEG, LAT), BF16), VMEM((own, LAT, DEG), BF16),
            VMEM((D, 2 * C, 2 * C), BF16),
            VMEM((LAT * 2 * own, C), F32),
            VMEM((2, DEG * chunk_modes(own) * 2, C), F32),
            VMEM((J, KD, C), F32), VMEM((J, KD, C), BF16),
            DMA((L,)), DMA((3,)), DMA, DMA((L, R)), DMA((L, R)),
            DMA((2,)), DMA((2,)), DMA((L, R)), DMA((L, R)),
            DMA((own, G)), DMA((own, G)), DMA((own, G)), DMA((own, G)),
        ],
        compiler_params=pltpu.CompilerParams(
            collective_id=0, has_side_effects=True, vmem_limit_bytes=60 * 1024 * 1024
        ),
    )(state, mix_weight, skip_weight)


def solution(mesh):
    placed = (P(None, "lat", "lon", None), P("lat", None, None, None), P())
    return jax.shard_map(
        shards, mesh=mesh, in_specs=placed, out_specs=P(None, "lat", "lon", None), check_vma=False
    )
```

```python
import functools
import math

import jax
import jax.numpy as jnp
from jax import lax
from jax.experimental import pallas as pl
from jax.experimental.pallas import tpu as pltpu
from jax.sharding import PartitionSpec as P

MESH = pl.DeviceIdType.MESH
rescale_limit = 1e18
log_rescale = 18.0 * math.log(10.0)
F32 = jnp.float32
BF16 = jnp.bfloat16


def repeat(first, last, body):
    if last - first > 64:
        lax.fori_loop(first, last, body, 0)
    else:
        for index in range(first, last):
            body(index, 0)


def ring(value, count):
    return jnp.where(value >= count, value - count, value)


def modulo(value, size):
    return value & (size - 1) if size & (size - 1) == 0 else lax.rem(value, size)


def build_forward(ft, lon_count, own, block):
    rows, columns = ft.shape
    quarter = lon_count // 4
    devices = rows // 2 // own

    def fill(step, carry):
        start = pl.multiple_of(step * block, block)
        q = lax.broadcasted_iota(jnp.int32, (block, columns), 0) + start
        k = lax.broadcasted_iota(jnp.int32, (block, columns), 1)
        mode = modulo(q >> 1, own) * devices + lax.div(q >> 1, own)
        phase = modulo(k * mode + (q & 1) * quarter, lon_count)
        folded = quarter - jnp.minimum(phase, lon_count - phase)
        angle = folded.astype(F32) * (2.0 * math.pi / lon_count)
        square = angle * angle
        total = jnp.full_like(square, 1.0 / math.factorial(13))
        for power in (11, 9, 7, 5, 3, 1):
            sign = 1.0 if power % 4 == 1 else -1.0
            total = total * square + sign / math.factorial(power)
        ft[pl.ds(start, block), :] = (total * angle * (1.0 / math.sqrt(lon_count))).astype(BF16)
        return carry

    lax.fori_loop(0, rows // block, fill, 0)


def build_backward(bt, ft, block):
    rows = ft.shape[0]
    for start in range(0, rows, block):
        bt[:, start : start + block] = jnp.transpose(ft[start : start + block, :].astype(F32)).astype(BF16)


def build_legendre(lg, an, syt, first_mode, stride):
    own, degrees, lat_count = lg.shape
    shape = (own, lat_count)
    position = lax.broadcasted_iota(jnp.int32, (1, lat_count), 1).astype(F32)
    colatitude = math.pi * (position + 0.5) / lat_count
    cosine = jnp.cos(colatitude)
    sine = jnp.sin(colatitude)
    orders = (lax.broadcasted_iota(jnp.int32, shape, 0) * stride + first_mode).astype(F32)
    counter = (lax.broadcasted_iota(jnp.int32, (own, degrees), 1) + 1).astype(F32)
    own_order = (lax.broadcasted_iota(jnp.int32, (own, degrees), 0) * stride + first_mode).astype(F32)
    halves = 0.5 * jnp.log((2.0 * counter + 1.0) / (2.0 * counter))
    summed = jnp.sum(jnp.where(counter <= own_order, halves, 0.0), axis=1, keepdims=True)
    log_start = 0.5 * math.log(0.5) + summed + orders * jnp.log(sine)
    squares = orders * orders
    wide_cosine = jnp.broadcast_to(cosine, shape)
    unroll = 8

    def advance(step, carry):
        previous, earlier, exponent = carry
        for offset in range(unroll):
            index = step * unroll + offset
            level = jnp.full(shape, index, jnp.int32).astype(F32)
            ratio_a = jnp.sqrt(
                jnp.maximum(4.0 * level * level - 1.0, 0.0) / jnp.maximum(level * level - squares, 1.0)
            )
            below = level - 1.0
            ratio_b = jnp.sqrt(
                jnp.maximum(below * below - squares, 0.0)
                / jnp.maximum(4.0 * below * below - 1.0, 1.0)
            )
            raised = ratio_a * (wide_cosine * previous - ratio_b * earlier)
            at_start = level == orders
            current = jnp.where(at_start, 1.0, jnp.where(level > orders, raised, 0.0))
            exponent = jnp.where(at_start, log_start, exponent)
            oversize = jnp.abs(current) > rescale_limit
            factor = jnp.where(oversize, 1.0 / rescale_limit, 1.0)
            earlier = previous * factor
            previous = current * factor
            exponent = exponent + jnp.where(oversize, log_rescale, 0.0)
            value = previous * jnp.exp(exponent)
            for i in range(own):
                lg[i, pl.ds(index, 1), :] = value[i : i + 1]
        return previous, earlier, exponent

    zeros = jnp.zeros(shape, F32)
    lax.fori_loop(0, degrees // unroll, advance, (zeros, zeros, zeros))
    for i in range(own):
        value = lg[i]
        an[i] = (value * (math.pi / math.sqrt(lat_count)) * sine).astype(BF16)
        weight = jnp.where(orders[i : i + 1] == 0.0, 1.0, 2.0)
        syt[i] = jnp.transpose((value * (1.0 / math.sqrt(degrees))) * weight).astype(BF16)


def chunk_modes(own):
    return own // 2 if own % 2 == 0 else own


def gelu(v):
    return 0.5 * v * (1.0 + jnp.tanh(math.sqrt(2.0 / math.pi) * (v + 0.044715 * v * v * v)))


def kernel(
    L, G, state, mix, skip, out,
    st, mx, sk, ra, sb, rb, sc, rc, sd, rd, se, re, sf, rf,
    ft, bt, lg, an, syt, wb, scr, scm, local, ov,
    sem_out, sem_in, sem_own, sem_a, sem_ra, sem_s, sem_r, sem_f, sem_rf,
    sem_cs, sem_cr, sem_ds, sem_dr,
):
    N = L * G
    J, KD, C = st.shape
    R = J // L
    D = mx.shape[0]
    K = KD * L
    own = lg.shape[0]
    Q = 2 * own * N
    LAT = J * G
    DEG = D * G
    a = lax.axis_index("lon")
    g = lax.axis_index("lat")
    n = g * L + a

    def place(p):
        return (lax.rem(p, L), p // L)

    loads = [
        pltpu.make_async_copy(state.at[0], st, sem_in.at[0]),
        pltpu.make_async_copy(mix, mx, sem_in.at[1]),
        pltpu.make_async_copy(skip, sk, sem_in.at[2]),
    ]
    rc[...] = jnp.zeros_like(rc)
    rd[...] = jnp.zeros_like(rd)
    barrier = pltpu.get_barrier_semaphore()

    def greet(off, carry):
        pl.semaphore_signal(barrier, inc=1, device_id=place(ring(n + off, N)), device_id_type=MESH)
        return carry

    repeat(1, N, greet)
    own_rows = pltpu.make_async_copy(state.at[0, pl.ds(a * R, R)], ra.at[a], sem_own)
    own_rows.start()
    for load in loads:
        load.start()
    pl.semaphore_wait(barrier, N - 1)

    def halves(split):
        step = R // 2 if split and R % 2 == 0 else R
        return [(s, pl.ds(s * step, step)) for s in range(R // step)]

    def spread(stage, src, dst, count, me, target, rows):
        def send(off, carry):
            p = ring(me + off, count)
            pltpu.make_async_remote_copy(
                src_ref=src.at[p, rows], dst_ref=dst.at[me, rows],
                send_sem=sem_s.at[stage], recv_sem=sem_r.at[stage],
                device_id=target(p), device_id_type=MESH,
            ).start()
            return carry

        repeat(1, count, send)
        dst[me, rows] = src[me, rows]

    def gathered(stage, dst, count, rows):
        part = dst.at[pl.ds(0, count - 1), rows]
        pltpu.make_async_copy(part, part, sem_r.at[stage]).wait()

    def drained(stage, src, count, rows):
        part = src.at[pl.ds(0, count - 1), rows]
        pltpu.make_async_copy(part, part, sem_s.at[stage]).wait()

    def row_copy(off, r):
        b = lax.rem(a + off, L)
        return pltpu.make_async_remote_copy(
            src_ref=state.at[0, b * R + r], dst_ref=ra.at[a, r],
            send_sem=sem_a.at[off, r], recv_sem=sem_ra.at[off, r],
            device_id=(b, g), device_id_type=MESH,
        )

    for r in range(R):
        for off in range(1, L):
            row_copy(off, r).start()
    build_forward(ft, K, own, 32)
    own_rows.wait()
    for r in range(R):
        for off in range(1, L):
            row_copy(off, r).wait_recv()
        rows = ra[:, r].reshape(K, C)
        spectrum = jnp.dot(ft[...], rows, preferred_element_type=F32)
        sb[:, r] = spectrum.reshape(N, 2 * own, C).astype(BF16)
        for s, part_rows in halves(True):
            if r == part_rows.start + part_rows.size - 1:
                spread(s, sb, rb, N, n, place, part_rows)

    def wanted(i, h, d):
        return N * i + h * L + a <= D * d + D - 1

    def forth(i, h):
        return pltpu.make_async_remote_copy(
            src_ref=sc.at[i, h], dst_ref=rc.at[i, g],
            send_sem=sem_cs.at[i, h], recv_sem=sem_cr.at[i, g],
            device_id=(a, h), device_id_type=MESH,
        )

    def came_forth(i, h):
        return pltpu.make_async_copy(rc.at[i, h], rc.at[i, h], sem_cr.at[i, h])

    def went_forth(i, h):
        return pltpu.make_async_copy(sc.at[i, h], sc.at[i, h], sem_cs.at[i, h])

    def back(i, h):
        return pltpu.make_async_remote_copy(
            src_ref=sd.at[i, h], dst_ref=rd.at[i, g],
            send_sem=sem_ds.at[i, h], recv_sem=sem_dr.at[i, g],
            device_id=(a, h), device_id_type=MESH,
        )

    def came_back(i, h):
        return pltpu.make_async_copy(rd.at[i, h], rd.at[i, h], sem_dr.at[i, h])

    def went_back(i, h):
        return pltpu.make_async_copy(sd.at[i, h], sd.at[i, h], sem_ds.at[i, h])

    def start(copy, i, condition):
        def act(h):
            @pl.when(condition(h))
            def _():
                copy(i, h).start()
        return act

    def finish(copy, i, condition):
        def act(h):
            @pl.when(condition(h))
            def _():
                copy(i, h).wait()
        return act

    def each_other(act):
        def step(off, carry):
            act(ring(g + off, G))
            return carry

        repeat(1, G, step)

    build_legendre(lg, an, syt, n, N)
    for s, part_rows in halves(True):
        gathered(s, rb, N, part_rows)
    scr[...] = rb[...].astype(F32).reshape(LAT * 2 * own, C)
    for i in range(own):
        pieces = jnp.concatenate(
            [scr[pl.ds(2 * i + part, LAT, stride=2 * own), :] for part in range(2)], axis=1
        ).astype(BF16)
        coeffs = jnp.dot(an[i], pieces, preferred_element_type=F32)
        for part in range(2):
            sc[i, :, part] = coeffs[:, part * C : (part + 1) * C].reshape(G, D, C).astype(BF16)
        each_other(start(forth, i, lambda h: wanted(i, g, h)))
        rc[i, g] = sc[i, g]

    for load in loads:
        load.wait()
    for l in range(D):
        wb[l, :C, :C] = mx[l, 0]
        wb[l, :C, C:] = mx[l, 1]
        wb[l, C:, :C] = -mx[l, 1]
        wb[l, C:, C:] = mx[l, 0]
    size = chunk_modes(own)
    for first in range(0, own, size):
        for i in range(first, first + size):
            each_other(finish(came_forth, i, lambda h: wanted(i, h, g)))
        scm[0] = rc[first : first + size].astype(F32).reshape(size * G * 2 * D, C)
        for l in range(D):
            paired = jnp.concatenate(
                [scm[0, pl.ds(part * D + l, size * G, stride=2 * D), :] for part in range(2)], axis=1
            ).astype(BF16)
            mixed = jnp.dot(paired, wb[l], preferred_element_type=F32)
            for part in range(2):
                scm[1, pl.ds(part * D + l, size * G, stride=2 * D), :] = mixed[:, part * C : (part + 1) * C]
        sd[first : first + size] = scm[1].reshape(size, G, 2, D, C).astype(BF16)
        for i in range(first, first + size):
            each_other(start(back, i, lambda h: wanted(i, h, g)))
            rd[i, g] = sd[i, g]

    for j in range(J):
        local[j] = jnp.dot(st[j], sk[...], preferred_element_type=F32)
    build_backward(bt, ft, 128)
    for i in range(own):
        each_other(finish(came_back, i, lambda h: wanted(i, g, h)))
        pieces = jnp.concatenate([rd[i, :, part].reshape(DEG, C) for part in range(2)], axis=1)
        gridded = jnp.dot(syt[i], pieces, preferred_element_type=F32)
        for part in range(2):
            scr[pl.ds(2 * i + part, LAT, stride=2 * own), :] = gridded[:, part * C : (part + 1) * C]
    se[...] = scr[...].reshape(N, R, 2 * own, C).astype(BF16)

    for s, part_rows in halves(True):
        spread(2 + s, se, re, N, n, place, part_rows)

    def sector_copy(off, r):
        b = lax.rem(a + off, L)
        return pltpu.make_async_remote_copy(
            src_ref=sf.at[b, r], dst_ref=rf.at[a, r],
            send_sem=sem_f.at[off, r], recv_sem=sem_rf.at[off, r],
            device_id=(b, g), device_id_type=MESH,
        )

    def inverse(b, r):
        table = bt[pl.ds(pl.multiple_of(b * KD, KD), KD), :]
        modes = re[:, r].reshape(Q, C)
        return jnp.dot(table, modes, preferred_element_type=F32).astype(BF16)

    def result_copy(off, b):
        rows = pl.ds(b * R, R)
        return pltpu.make_async_copy(ov.at[rows], out.at[0, rows], sem_out.at[off])

    for r in range(R):
        for s, part_rows in halves(True):
            if r == part_rows.start:
                gathered(2 + s, re, N, part_rows)
        for off in range(1, L):
            b = lax.rem(a + off, L)
            sf[b, r] = inverse(b, r)
            sector_copy(off, r).start()
    for r in range(R):
        row = a * R + r
        ov[row] = gelu(inverse(a, r).astype(F32) + local[row]).astype(BF16)
    result_copy(0, a).start()
    for off in range(1, L):
        b = lax.rem(a + L - off, L)
        for r in range(R):
            sector_copy(off, r).wait_recv()
            row = b * R + r
            ov[row] = gelu(rf[b, r].astype(F32) + local[row]).astype(BF16)
        result_copy(off, b).start()

    for r in range(R):
        for off in range(1, L):
            row_copy(off, r).wait_send()
            sector_copy(off, r).wait_send()
    for off in range(L):
        result_copy(off, lax.rem(a + L - off, L)).wait()
    for s, part_rows in halves(True):
        drained(s, sb, N, part_rows)
    for i in range(own):
        each_other(finish(went_forth, i, lambda h: wanted(i, g, h)))
        each_other(finish(went_back, i, lambda h: wanted(i, h, g)))
    for s, part_rows in halves(True):
        drained(2 + s, se, N, part_rows)


def shards(state, mix_weight, skip_weight):
    samples, J, KD, C = state.shape
    D = mix_weight.shape[0]
    L = lax.axis_size("lon")
    G = lax.axis_size("lat")
    N, R, K, LAT, DEG = L * G, J // L, KD * L, J * G, D * G
    own = K // 2 // N
    Q = 2 * own * N
    wide = (N, R, 2 * own, C)
    deep = (own, G, 2, D, C)
    VMEM = pltpu.VMEM
    DMA = pltpu.SemaphoreType.DMA
    return pl.pallas_call(
        functools.partial(kernel, L, G),
        out_shape=jax.ShapeDtypeStruct(state.shape, BF16),
        in_specs=[pl.BlockSpec(memory_space=pltpu.HBM)] * 3,
        out_specs=pl.BlockSpec(memory_space=pltpu.VMEM),
        scratch_shapes=[
            VMEM((J, KD, C), BF16),
            VMEM(mix_weight.shape, BF16),
            VMEM((C, C), BF16),
            VMEM((L, R, KD, C), BF16),
            VMEM(wide, BF16), VMEM(wide, BF16),
            VMEM(deep, BF16), VMEM(deep, BF16),
            VMEM(deep, BF16), VMEM(deep, BF16),
            VMEM(wide, BF16), VMEM(wide, BF16),
            VMEM((L, R, KD, C), BF16), VMEM((L, R, KD, C), BF16),
            VMEM((Q, K), BF16), VMEM((K, Q), BF16),
            VMEM((own, DEG, LAT), F32),
            VMEM((own, DEG, LAT), BF16), VMEM((own, LAT, DEG), BF16),
            VMEM((D, 2 * C, 2 * C), BF16),
            VMEM((LAT * 2 * own, C), F32),
            VMEM((2, DEG * chunk_modes(own) * 2, C), F32),
            VMEM((J, KD, C), F32), VMEM((J, KD, C), BF16),
            DMA((L,)), DMA((3,)), DMA, DMA((L, R)), DMA((L, R)),
            DMA((4,)), DMA((4,)), DMA((L, R)), DMA((L, R)),
            DMA((own, G)), DMA((own, G)), DMA((own, G)), DMA((own, G)),
        ],
        compiler_params=pltpu.CompilerParams(
            collective_id=0, has_side_effects=True, vmem_limit_bytes=60 * 1024 * 1024
        ),
    )(state, mix_weight, skip_weight)


def solution(mesh):
    placed = (P(None, "lat", "lon", None), P("lat", None, None, None), P())
    return jax.shard_map(
        shards, mesh=mesh, in_specs=placed, out_specs=P(None, "lat", "lon", None), check_vma=False
    )
```
